32 devices in a mesh: pb: 4 (over y, core), kv: 4 (over z), ex: 2 (over x).
Axes of the slice: x: 2, y: 2, z: 4, core: 2. Of those that a mesh axis runs over, the one named last changes fastest.
Arguments:
- queries: bfloat16 [8, 8192, 256], P(('pb', 'ex'), 'kv'), may hold values from -6 to 6
- coords: float32 [8, 3, 8192], P(('pb', 'ex'), None, 'kv'), may hold values from -1 to 1
- inputs: bfloat16 [8, 2048, 256], P(('pb', 'ex'), 'kv'), may hold values from -10 to 10
- w_query: bfloat16 [256, 256], replicated, may hold values from -0.375 to 0.375
- w_key: bfloat16 [256, 256], replicated, may hold values from -0.375 to 0.375
- w_value: bfloat16 [256, 256], replicated, may hold values from -0.375 to 0.375
- w_out: bfloat16 [256, 256], replicated, may hold values from -0.375 to 0.375
- expert_in: bfloat16 [8, 256, 1024], P('ex', ('pb', 'kv')), may hold values from -0.375 to 0.375
- expert_out: bfloat16 [8, 1024, 256], P('ex', ('pb', 'kv')), may hold values from -0.1875 to 0.1875
- gate_geo: float32 [8, 3], replicated, may hold values from -6 to 6
- routes: int32 [8, 64, 1], P(('pb', 'ex'), 'kv'), may hold values from 0 to 7; in each aligned block of 16 rows (0 to 15, 16 to 31, ..., all dimensions but the last counted through in order) at most 3 rows name the same one
Outputs:
- result: bfloat16 [8, 8192, 256], P(('pb', 'ex'), 'kv')
The draws below stay inside these ranges and needn't reach their ends.
Inputs may be any that keep to these rules, and one draw needn't show every extreme that they name: `routes`: in each aligned block of 16 tiles (the tiles of one device) no expert is named by more than 3 tiles, a bound that some block reaches.
All inputs are finite; a program needn't handle non-finite values.
Results may differ from the reference program's by a relative error of at most 0.0053.
Values may be sent and summed in bfloat16 or wider, within the bound.
A program may use at most 64 MiB of HBM per device.

```python
import math
import jax
import jax.numpy as jnp
import numpy as np
from jax import lax

D = 256
H = 8
DH = 32
F = 1024
E = 8
TILE = 128
CAP = 3
TILES_DEV = 16
IN_DEV = 512
SAMPLES = 8
TILES = 64
QPTS = 8192
INPTS = 2048


def draw_inputs(key, part):
    noise_key, offset_key = jax.random.split(key, 2)
    blocks = INPTS // IN_DEV
    offset = jnp.clip(jax.random.normal(offset_key, (SAMPLES, blocks, 1, D), jnp.float32), -3.0, 3.0)
    offset = jnp.broadcast_to(offset, (SAMPLES, blocks, IN_DEV, D)).reshape(SAMPLES, INPTS, D)
    noise = jnp.clip(jax.random.normal(noise_key, (SAMPLES, INPTS, D), jnp.float32), -4.0, 4.0)
    return (noise + 1.5 * offset).astype(jnp.bfloat16)


def block_scale(rng, extent, pieces, low, largest):
    loudness, own = 1.0, jax.random.fold_in(rng, 6)
    for position, shards_of in pieces:
        draws = jnp.exp(jax.random.uniform(jax.random.fold_in(own, position), (shards_of,), jnp.float32, low / len(pieces), largest / len(pieces)))
        loudness = loudness * jnp.repeat(draws, extent[position] // shards_of).reshape([-1 if axis == position else 1 for axis in range(len(extent))])
    return loudness


def routed_block(rng, own, number, rows, count, top, bound, slope):
    ranking = jax.random.permutation(rng, count)
    crowded, usual = load_shares(count, rows * top, bound, slope, True), load_shares(count, rows * top, bound, slope, False)
    places = jnp.arange(count)

    def named(sizes, rotation):
        used = int((sizes > 0).sum())
        fixed = max(1, used // 4)
        shifted = fixed + (places - fixed + rotation * (used - fixed)) % max(1, count - fixed)
        return jnp.zeros((count,), jnp.int32).at[ranking[jnp.where(places < fixed, places, shifted)]].set(jnp.asarray(sizes, jnp.int32))

    sizes = jnp.where(number % 4 == 0, named(crowded, number // 4), named(usual, number - number // 4 - 1))
    mixed = jax.random.permutation(jax.random.fold_in(own, 3), count)
    giver, taker = mixed[0:count // 2 * 2:2], mixed[1:count // 2 * 2:2]
    slack = jnp.minimum(sizes[giver] - 1, bound - sizes[taker]) // 2
    slack = jnp.where((giver == ranking[0]) | (taker == ranking[0]) | (sizes[taker] == 0), 0, jnp.maximum(slack, 0))
    shifted = jax.random.randint(jax.random.fold_in(own, 4), (count // 2,), 0, 1 << 20) % (slack + 1)
    sizes = sizes.at[giver].add(-shifted).at[taker].add(shifted)
    items = jnp.searchsorted(jnp.cumsum(sizes), jnp.arange(rows * top), side="right").astype(jnp.int32)
    table = items.reshape(top, rows).T
    table = table[jax.random.permutation(jax.random.fold_in(own, 1), rows)]
    rotation = jax.random.randint(jax.random.fold_in(own, 2), (rows, 1), 0, top)
    return jnp.take_along_axis(table, (jnp.arange(top)[None, :] + rotation) % top, axis=1)


def load_shares(count, total, bound, slope, full):
    portions = [(1 << 20) // math.isqrt(rank ** slope) + 1 for rank in range(1, count + 1)]
    largest = bound if full else min(bound, max(-(-total // count), total * portions[0] // sum(portions)))
    least = 1 if total - largest >= count - 1 else 0
    holding, rest = [largest] + [least] * (count - 1), total - largest - least * (count - 1)
    while rest > 0:
        free = [i for i in range(1, count) if holding[i] < largest] or [i for i in range(1, count) if holding[i] < bound]
        whole, left = sum([portions[i] for i in free]), rest
        for i in free:
            addition = min(bound - holding[i], max(1, left * portions[i] // whole), rest)
            holding[i] = holding[i] + addition
            rest = rest - addition
    return np.array(holding)


def bell_draw(own_key, extent, width, limit, cuts=(), dtype=jnp.bfloat16):
    level = block_scale(own_key, extent, cuts, -0.22, 0.18) if cuts else 1.0
    values = jax.random.normal(own_key, extent, jnp.float32) * width * level
    return jnp.minimum(jnp.maximum(values, -limit), limit).astype(dtype)


def setup_inputs(seed: int = 0) -> dict:
    streams_of = jax.random.split(jax.random.key(seed), 12)
    queries = bell_draw(streams_of[0], (SAMPLES, QPTS, D), 1.0, 6.0, ((0, 8), (1, 4)))
    coords = jnp.clip(jax.random.uniform(streams_of[1], (SAMPLES, 3, QPTS), jnp.float32, -1.0, 1.0) * block_scale(streams_of[1], (SAMPLES, 3, QPTS), ((0, 8), (2, 4)), -0.4, 0.0), -1.0, 1.0)
    inputs = draw_inputs(jax.random.fold_in(streams_of[11], 71), 0)
    w_query = bell_draw(streams_of[3], (D, D), D ** -0.5, 0.375)
    w_key = bell_draw(streams_of[4], (D, D), D ** -0.5, 0.375)
    w_value = bell_draw(streams_of[5], (D, D), D ** -0.5, 0.375)
    w_out = bell_draw(streams_of[6], (D, D), D ** -0.5, 0.375)
    expert_in = bell_draw(streams_of[7], (E, D, F), D ** -0.5, 0.375, ((0, 2), (1, 16)))
    expert_out = bell_draw(streams_of[8], (E, F, D), F ** -0.5, 0.1875, ((0, 2), (1, 16)))
    gate_geo = bell_draw(streams_of[9], (E, 3), 1.5, 6.0, (), jnp.float32)
    routes_keys = jax.random.split(jax.random.fold_in(streams_of[10], 1), SAMPLES * TILES // TILES_DEV)
    routes_turns = jax.random.permutation(jax.random.fold_in(streams_of[10], 3), SAMPLES * TILES // TILES_DEV)
    routes = jax.vmap(lambda own, number: routed_block(jax.random.fold_in(streams_of[10], 2), own, number, TILES_DEV, E, 1, CAP, 2))(routes_keys, routes_turns).reshape((SAMPLES, TILES, 1))
    return {"queries": queries, "coords": coords, "inputs": inputs, "w_query": w_query, "w_key": w_key, "w_value": w_value, "w_out": w_out, "expert_in": expert_in, "expert_out": expert_out, "gate_geo": gate_geo, "routes": routes}


def normalize(rows):
    rows = rows.astype(jnp.float32)
    centre = rows - lax.optimization_barrier(jnp.mean(rows, axis=-1, keepdims=True))
    return centre * lax.rsqrt(lax.optimization_barrier(jnp.mean(centre * centre, axis=-1, keepdims=True)) + 1e-05)

def feature(values):
    return jax.nn.elu(values) + 1.0

def reference(queries, coords, inputs, w_query, w_key, w_value, w_out, expert_in, expert_out, gate_geo, routes):
    high = lax.Precision.HIGHEST

    def one_sample(packed):
        query_rows, coord_rows, input_rows, route_rows = packed
        normed_in = normalize(input_rows).astype(jnp.bfloat16)
        keys = feature(jnp.dot(normed_in, w_key, preferred_element_type=jnp.float32)).reshape(INPTS, H, DH)
        vals = jnp.dot(normed_in, w_value, preferred_element_type=jnp.float32).reshape(INPTS, H, DH)
        memory = jnp.einsum('nhi,nhj->hij', keys, vals, precision=high)
        ksum = lax.optimization_barrier(jnp.sum(keys, axis=0))
        normed_q = normalize(query_rows).astype(jnp.bfloat16)
        qfeat = feature(jnp.dot(normed_q, w_query, preferred_element_type=jnp.float32)).reshape(QPTS, H, DH)
        numer = jnp.einsum('nhi,hij->nhj', qfeat, memory, precision=high)
        denom = jnp.einsum('nhi,hi->nh', qfeat, ksum, precision=high)
        attn = (numer / denom[:, :, None]).reshape(QPTS, D).astype(jnp.bfloat16)
        resid = (query_rows.astype(jnp.float32) + jnp.dot(attn, w_out, preferred_element_type=jnp.float32)).astype(jnp.bfloat16)
        normed_h = normalize(resid).astype(jnp.bfloat16).reshape(TILES, TILE, D)
        experts = route_rows[:, 0].astype(jnp.int32)

        def one_tile(item):
            rows, expert = item
            hidden = jax.nn.gelu(jnp.dot(rows, expert_in[expert], preferred_element_type=jnp.float32), approximate=False).astype(jnp.bfloat16)
            return jnp.dot(hidden, expert_out[expert], preferred_element_type=jnp.float32).astype(jnp.bfloat16)
        ffn = lax.map(one_tile, (normed_h, experts)).reshape(QPTS, D)
        coeff = gate_geo[experts]
        logit = lax.optimization_barrier(jnp.sum(coord_rows.reshape(3, TILES, TILE) * jnp.transpose(coeff)[:, :, None], axis=0)).reshape(QPTS)
        gate = jax.nn.sigmoid(logit)
        return (resid.astype(jnp.float32) + gate[:, None] * ffn.astype(jnp.float32)).astype(jnp.bfloat16)
    return lax.map(one_sample, (queries, coords, inputs, routes))
```

```python
import functools

import jax
import jax.numpy as jnp
from jax import lax
from jax.experimental import pallas as pl
from jax.experimental.pallas import tpu as pltpu
from jax.sharding import PartitionSpec as P

D = 256
H = 8
DH = 32
TILE = 128
CAP = 3


def normalize(rows):
    rows = rows.astype(jnp.float32)
    centre = rows - jnp.mean(rows, axis=-1, keepdims=True)
    return centre * lax.rsqrt(jnp.mean(centre * centre, axis=-1, keepdims=True) + 1e-05)


def feature(values):
    return jax.nn.elu(values) + 1.0


def fetch_rows(expert_in, expert_out):
    return (
        lax.all_gather(expert_in, ("pb", "kv"), axis=1, tiled=True),
        lax.all_gather(expert_out, ("pb", "kv"), axis=1, tiled=True),
    )


def body(
    queries, coords, inputs, w_query, w_key, w_value, w_out, expert_in, expert_out, gate_geo, routes
):
    high = lax.Precision.HIGHEST
    query_rows = queries[0]
    count = query_rows.shape[0]
    tiles_here = count // TILE
    normed_in = normalize(inputs[0]).astype(jnp.bfloat16)
    points = normed_in.shape[0]
    keys = feature(jnp.dot(normed_in, w_key, preferred_element_type=jnp.float32)).reshape(
        points, H, DH
    )
    vals = jnp.dot(normed_in, w_value, preferred_element_type=jnp.float32).reshape(points, H, DH)
    memory, ksum = lax.psum(
        (jnp.einsum("nhi,nhj->hij", keys, vals, precision=high), jnp.sum(keys, axis=0)), "kv"
    )
    normed_q = normalize(query_rows).astype(jnp.bfloat16)
    qfeat = feature(jnp.dot(normed_q, w_query, preferred_element_type=jnp.float32)).reshape(
        count, H, DH
    )
    numer = jnp.einsum("nhi,hij->nhj", qfeat, memory, precision=high)
    denom = jnp.einsum("nhi,hi->nh", qfeat, ksum, precision=high)
    attn = (numer / denom[:, :, None]).reshape(count, D).astype(jnp.bfloat16)
    resid = (
        query_rows.astype(jnp.float32) + jnp.dot(attn, w_out, preferred_element_type=jnp.float32)
    ).astype(jnp.bfloat16)
    experts = routes[0, :, 0]
    total_experts = gate_geo.shape[0]
    served = expert_in.shape[0]
    owners = total_experts // served
    onehot = (experts[:, None] == jnp.arange(total_experts, dtype=jnp.int32)[None, :]).astype(
        jnp.int32
    )
    before = jnp.cumsum(onehot, axis=0) - onehot
    rank = jnp.sum(before * onehot, axis=1)
    slot = experts * CAP + rank
    slots_all = total_experts * CAP
    select = (slot[None, :] == jnp.arange(slots_all, dtype=jnp.int32)[:, None]).astype(jnp.bfloat16)
    packed = jnp.dot(
        select, resid.reshape(tiles_here, TILE * D), preferred_element_type=jnp.float32
    ).astype(jnp.bfloat16)
    received = lax.all_to_all(packed, "ex", split_axis=0, concat_axis=0, tiled=True)
    arranged = received.reshape(owners, served, CAP * TILE, D)
    first_layer, second_layer = fetch_rows(expert_in, expert_out)
    outputs = []
    for local in range(served):
        rows = arranged[:, local].reshape(owners * CAP * TILE, D)
        rows = normalize(rows).astype(jnp.bfloat16)
        hidden = jax.nn.gelu(
            jnp.dot(rows, first_layer[local], preferred_element_type=jnp.float32), approximate=False
        ).astype(jnp.bfloat16)
        answer = jnp.dot(hidden, second_layer[local], preferred_element_type=jnp.float32).astype(
            jnp.bfloat16
        )
        outputs.append(answer.reshape(owners, 1, CAP * TILE, D))
    served_out = jnp.concatenate(outputs, axis=1).reshape(slots_all, TILE * D)
    returned = lax.all_to_all(served_out, "ex", split_axis=0, concat_axis=0, tiled=True)
    ffn = jnp.dot(jnp.transpose(select), returned, preferred_element_type=jnp.float32).reshape(
        count, D
    )
    coeff = jnp.dot(onehot.astype(jnp.float32), gate_geo, precision=high)
    logit = jnp.sum(
        coords[0].reshape(3, tiles_here, TILE) * jnp.transpose(coeff)[:, :, None], axis=0
    ).reshape(count)
    gate = jax.nn.sigmoid(logit)
    result = (resid.astype(jnp.float32) + gate[:, None] * ffn).astype(jnp.bfloat16)
    return result[None]


def gelu_exact(x):
    size = jnp.abs(x)
    t = 1.0 / (1.0 + 0.2316418882663604 * size)
    poly = t * (
        0.127414796 + t * (-0.142248368 + t * (0.710706871 + t * (-0.726576014 + t * 0.530702715)))
    )
    return jnp.maximum(x, 0.0) - size * poly * jnp.exp(-0.5 * x * x)


def phi(t):
    return jnp.where(t > 0.0, t + 1.0, jnp.exp(jnp.minimum(t, 0.0)))


def row_norm(rows):
    rows = rows.astype(jnp.float32)
    width = rows.shape[-1]
    centre = rows - jnp.sum(rows, axis=-1, keepdims=True) * (1.0 / width)
    var = jnp.sum(centre * centre, axis=-1, keepdims=True) * (1.0 / width)
    return (centre * lax.rsqrt(var + 1e-05)).astype(jnp.bfloat16)


def dot32(a, b):
    return jnp.dot(a, b, preferred_element_type=jnp.float32)


def fused(
    npb, nkv, nex,
    q_ref, coords_ref, in_ref, wq_ref, wk_ref, wv_ref, wo_ref, ein_ref, eout_ref, geo_ref, routes_ref,
    o_ref,
    w1, w2, qf, resid, normed, hidden, msg, kvbd, ksum,
    own_sem, zs, zr, ys, yr, xs, xr, fxs, fxr, fys, fyr, cs, cr, ms, mr,
):
    P_, Z, X = lax.axis_index("pb"), lax.axis_index("kv"), lax.axis_index("ex")
    py = lax.rem(P_ + 2, 4)
    pc = P_ + 1 - 2 * lax.rem(P_, 2)
    pcy = lax.rem(pc + 2, 4)
    xn = 1 - X
    bufs, srcs = (w1, w2), (ein_ref, eout_ref)
    served = ein_ref.shape[0]
    hs = served // 2
    to_y, to_x, to_c = {"pb": py}, {"ex": xn}, {"pb": pc}

    def block(m, x, p, z, half=None):
        if half is None:
            return bufs[m].at[pl.ds(x * served, served), p, z]
        return bufs[m].at[pl.ds(x * served + half * hs, hs), p, z]

    def rcopy(src, dst, s, r, dev):
        return pltpu.make_async_remote_copy(
            src_ref=src, dst_ref=dst, send_sem=s, recv_sem=r,
            device_id=dev, device_id_type=pl.DeviceIdType.MESH,
        )

    def zof(d):
        return lax.rem(Z + nkv - d, nkv)

    barrier = pltpu.get_barrier_semaphore()
    partners = [to_y, to_x, to_c] + [{"kv": lax.rem(Z + d, nkv)} for d in range(1, nkv)]
    for dev in partners:
        pl.semaphore_signal(barrier, inc=1, device_id=dev, device_id_type=pl.DeviceIdType.MESH)
    pl.semaphore_wait(barrier, len(partners))

    def own_copy(m):
        return pltpu.make_async_copy(srcs[m], block(m, X, P_, Z), own_sem.at[m])

    def z_copy(m, d):
        return rcopy(srcs[m], block(m, X, P_, Z), zs.at[m, d], zr.at[m, d], {"kv": lax.rem(Z + d, nkv)})

    def z_arrive(m, d):
        b = block(m, X, P_, zof(d))
        return rcopy(b, b, zs.at[m, d], zr.at[m, d], {"kv": lax.rem(Z + d, nkv)})

    def pair(m, x, p, d, s, r, dev, half=None, src=None):
        b = block(m, x, p, zof(d), half)
        return rcopy(b if src is None else src, b, s.at[m, d], r.at[m, d], dev)

    def core(m, k, d, src=None):
        x, p = ((X, P_), (X, py), (xn, P_), (xn, py))[k]
        b = block(m, x, p, zof(d))
        return rcopy(b if src is None else src, b, cs.at[m, k, d], cr.at[m, k, d], to_c)

    def core_arrive(m, k, d):
        x, p = ((X, pc), (X, pcy), (xn, pc), (xn, pcy))[k]
        b = block(m, x, p, zof(d))
        return rcopy(b, b, cs.at[m, k, d], cr.at[m, k, d], to_c)

    def start_z(m):
        own_copy(m).start()
        for d in range(1, nkv):
            z_copy(m, d).start()

    def start_xy(m):
        pair(m, X, P_, 0, xs, xr, to_x, src=srcs[m]).start()
        pair(m, X, P_, 0, ys, yr, to_y, src=srcs[m]).start()
        core(m, 0, 0, src=srcs[m]).start()

    def f1(m, d):
        z_arrive(m, d).wait_recv()
        pair(m, X, P_, d, xs, xr, to_x).start()
        pair(m, X, P_, d, ys, yr, to_y).start()
        core(m, 0, d).start()

    def f2(m, d):
        pair(m, X, py, d, ys, yr, to_y).wait_recv()
        pair(m, X, py, d, fxs, fxr, to_x, half=0).start()
        core(m, 1, d).start()
        pair(m, xn, P_, d, xs, xr, to_x).wait_recv()
        pair(m, xn, P_, d, fys, fyr, to_y, half=1).start()
        core(m, 2, d).start()

    def f3(m, d):
        pair(m, xn, py, d, fxs, fxr, to_x, half=0).wait_recv()
        pair(m, xn, py, d, fys, fyr, to_y, half=1).wait_recv()
        core(m, 3, d).start()

    def arrive_all(m):
        own_copy(m).wait()
        for d in range(nkv):
            for k in range(4):
                core_arrive(m, k, d).wait_recv()

    def sent_all(m):
        for d in range(nkv):
            if d:
                z_copy(m, d).wait_send()
            pair(m, X, P_, d, xs, xr, to_x).wait_send()
            pair(m, X, P_, d, ys, yr, to_y).wait_send()
            pair(m, X, py, d, fxs, fxr, to_x, half=0).wait_send()
            pair(m, xn, P_, d, fys, fyr, to_y, half=1).wait_send()
            for k in range(4):
                core(m, k, d).wait_send()

    start_z(0)
    start_xy(0)

    width = q_ref.shape[1]
    nin = row_norm(in_ref[...])
    keys = phi(dot32(nin, wk_ref[...]))
    vals = dot32(nin, wv_ref[...])
    keys_b, vals_b = keys.astype(jnp.bfloat16), vals.astype(jnp.bfloat16)
    lane = lax.broadcasted_iota(jnp.int32, (DH, 128), 1) // DH
    per = 128 // DH
    rows_kv = DH * (width // 128)
    for t in range(width // 128):
        cols = slice(128 * t, 128 * (t + 1))
        mem = lax.dot_general(
            keys_b[:, cols], vals_b[:, cols], (((0,), (0,)), ((), ())),
            preferred_element_type=jnp.float32,
        )
        total = jnp.zeros((DH, 128), jnp.float32)
        for h in range(per):
            total = jnp.where(lane == h, mem[h * DH : (h + 1) * DH], total)
        msg[0, DH * t : DH * (t + 1), :] = total
        sums = jnp.sum(keys[:, cols], axis=0, keepdims=True)
        msg[0, rows_kv + 8 * t : rows_kv + 8 * (t + 1), :] = jnp.broadcast_to(sums, (8, 128))

    def m_copy(d):
        return rcopy(msg.at[0], msg.at[d], ms.at[d], mr.at[d], {"kv": lax.rem(Z + d, nkv)})

    for d in range(1, nkv):
        m_copy(d).start()

    count = q_ref.shape[0]
    step = 256
    chunks = count // step

    def q_stage(lo, hi):
        @pl.loop(lo, hi)
        def _(i):
            rows = pl.ds(pl.multiple_of(i * step, step), step)
            qf[rows, :] = phi(dot32(row_norm(q_ref[rows, :]), wq_ref[...])).astype(jnp.bfloat16)

    part = chunks // 4
    f1(0, 1)
    q_stage(0, part)
    f1(0, 2)
    f2(0, 0)
    q_stage(part, 2 * part)
    f1(0, 3)
    start_z(1)
    f2(0, 1)
    q_stage(2 * part, chunks)

    for d in range(1, nkv):
        m_copy(d).wait_recv()
    both = msg[0]
    for d in range(1, nkv):
        both = both + msg[d]
    kvbd[...] = jnp.zeros_like(kvbd)
    for t in range(width // 128):
        mem = both[DH * t : DH * (t + 1)]
        for h in range(per):
            r0 = 128 * t + DH * h
            kvbd[r0 : r0 + DH, 128 * t : 128 * (t + 1)] = jnp.where(lane == h, mem, 0.0).astype(jnp.bfloat16)
        ksum[:, 128 * t : 128 * (t + 1)] = both[rows_kv + 8 * t : rows_kv + 8 * (t + 1)]
    same = (
        lax.broadcasted_iota(jnp.int32, (width, width), 0) // DH
        == lax.broadcasted_iota(jnp.int32, (width, width), 1) // DH
    ).astype(jnp.float32).astype(jnp.bfloat16)

    def attn_stage(lo, hi):
        @pl.loop(lo, hi)
        def _(i):
            rows = pl.ds(pl.multiple_of(i * step, step), step)
            f = qf[rows, :]
            numer = dot32(f, kvbd[...])
            denom = dot32((f.astype(jnp.float32) * ksum[0:1, :]).astype(jnp.bfloat16), same)
            attn = (numer / denom).astype(jnp.bfloat16)
            r = (q_ref[rows, :].astype(jnp.float32) + dot32(attn, wo_ref[...])).astype(jnp.bfloat16)
            resid[rows, :] = r
            normed[rows, :] = row_norm(r)

    attn_stage(0, part)
    f3(0, 0)
    f2(0, 2)
    attn_stage(part, 2 * part)
    f3(0, 1)
    f2(0, 3)
    start_xy(1)
    attn_stage(2 * part, chunks)
    f3(0, 2)
    f3(0, 3)
    f1(1, 1)
    arrive_all(0)

    tiles = count // TILE
    fdim = hidden.shape[1]
    wide = 256

    def up_stage(lo, hi):
        @pl.loop(lo, hi)
        def _(i):
            rows = pl.ds(pl.multiple_of(i * TILE, TILE), TILE)
            e = routes_ref[i, 0]
            x = normed[rows, :]
            for c in range(fdim // wide):
                w = w1[e, :, :, :, c * wide : (c + 1) * wide].reshape(width, wide)
                hidden[rows, c * wide : (c + 1) * wide] = gelu_exact(dot32(x, w)).astype(jnp.bfloat16)

    quarter = tiles // 8
    up_stage(0, quarter)
    f1(1, 2)
    f2(1, 0)
    up_stage(quarter, 2 * quarter)
    f1(1, 3)
    f2(1, 1)
    up_stage(2 * quarter, 4 * quarter)
    f3(1, 0)
    f2(1, 2)
    up_stage(4 * quarter, 6 * quarter)
    f3(1, 1)
    f2(1, 3)
    up_stage(6 * quarter, tiles)
    f3(1, 2)
    f3(1, 3)
    arrive_all(1)

    @pl.loop(0, tiles)
    def _(i):
        start = pl.multiple_of(i * TILE, TILE)
        rows = pl.ds(start, TILE)
        e = routes_ref[i, 0]
        ffn = dot32(hidden[rows, :], w2[e].reshape(fdim, width)).astype(jnp.bfloat16).astype(jnp.float32)
        logit = coords_ref[0:1, rows] * geo_ref[e, 0]
        logit = logit + coords_ref[1:2, rows] * geo_ref[e, 1]
        logit = logit + coords_ref[2:3, rows] * geo_ref[e, 2]
        gate = 1.0 / (1.0 + jnp.exp(-logit))
        gate = jnp.transpose(jnp.broadcast_to(gate, (TILE, TILE)))
        gate = jnp.concatenate([gate] * (width // TILE), axis=1)
        o_ref[rows, :] = (resid[rows, :].astype(jnp.float32) + gate * ffn).astype(jnp.bfloat16)

    sent_all(0)
    sent_all(1)
    for d in range(1, nkv):
        m_copy(d).wait_send()


def fused_body(npb, nkv, nex, queries, coords, inputs, w_query, w_key, w_value, w_out, expert_in, expert_out, gate_geo, routes):
    count, width = queries.shape[1:]
    served, rows1, fdim = expert_in.shape
    rows2 = expert_out.shape[1]
    total = served * nex
    vmem = pl.BlockSpec(memory_space=pltpu.VMEM)
    smem = pl.BlockSpec(memory_space=pltpu.SMEM)
    hbm = pl.BlockSpec(memory_space=pl.ANY)
    dma = pltpu.SemaphoreType.DMA
    bf = jnp.bfloat16
    out = pl.pallas_call(
        functools.partial(fused, npb, nkv, nex),
        out_shape=jax.ShapeDtypeStruct((count, width), bf),
        in_specs=[vmem] * 7 + [hbm] * 2 + [smem] * 2,
        out_specs=vmem,
        scratch_shapes=[
            pltpu.VMEM((total, npb, nkv, rows1, fdim), bf),
            pltpu.VMEM((total, npb, nkv, rows2, width), bf),
            pltpu.VMEM((count, width), bf),
            pltpu.VMEM((count, width), bf),
            pltpu.VMEM((count, width), bf),
            pltpu.VMEM((count, fdim), bf),
            pltpu.VMEM((nkv, (DH + 8) * (width // 128), 128), jnp.float32),
            pltpu.VMEM((width, width), bf),
            pltpu.VMEM((8, width), jnp.float32),
            dma((2,)),
        ] + [dma((2, nkv))] * 10 + [dma((2, 4, nkv))] * 2 + [dma((nkv,))] * 2,
        compiler_params=pltpu.CompilerParams(collective_id=0, has_side_effects=True),
        name="fused",
    )(queries[0], coords[0], inputs[0], w_query, w_key, w_value, w_out, expert_in, expert_out, gate_geo, routes[0])
    return out[None]


def solution(mesh):
    in_specs = (
        P(("pb", "ex"), "kv", None),
        P(("pb", "ex"), None, "kv"),
        P(("pb", "ex"), "kv", None),
        P(),
        P(),
        P(),
        P(),
        P("ex", ("pb", "kv"), None),
        P("ex", ("pb", "kv"), None),
        P(),
        P(("pb", "ex"), "kv", None),
    )
    out_specs = P(("pb", "ex"), "kv", None)
    npb, nkv, nex = (mesh.shape[a] for a in ("pb", "kv", "ex"))
    chosen = functools.partial(fused_body, npb, nkv, nex) if (npb, nex) == (4, 2) else body
    return jax.shard_map(chosen, mesh=mesh, in_specs=in_specs, out_specs=out_specs, check_vma=False)
```

```python
import functools

import jax
import jax.numpy as jnp
from jax import lax
from jax.experimental import pallas as pl
from jax.experimental.pallas import tpu as pltpu
from jax.sharding import PartitionSpec as P

D = 256
H = 8
DH = 32
TILE = 128
CAP = 3


def normalize(rows):
    rows = rows.astype(jnp.float32)
    centre = rows - jnp.mean(rows, axis=-1, keepdims=True)
    return centre * lax.rsqrt(jnp.mean(centre * centre, axis=-1, keepdims=True) + 1e-05)


def feature(values):
    return jax.nn.elu(values) + 1.0


def fetch_rows(expert_in, expert_out):
    return (
        lax.all_gather(expert_in, ("pb", "kv"), axis=1, tiled=True),
        lax.all_gather(expert_out, ("pb", "kv"), axis=1, tiled=True),
    )


def body(
    queries, coords, inputs, w_query, w_key, w_value, w_out, expert_in, expert_out, gate_geo, routes
):
    high = lax.Precision.HIGHEST
    query_rows = queries[0]
    count = query_rows.shape[0]
    tiles_here = count // TILE
    normed_in = normalize(inputs[0]).astype(jnp.bfloat16)
    points = normed_in.shape[0]
    keys = feature(jnp.dot(normed_in, w_key, preferred_element_type=jnp.float32)).reshape(
        points, H, DH
    )
    vals = jnp.dot(normed_in, w_value, preferred_element_type=jnp.float32).reshape(points, H, DH)
    memory, ksum = lax.psum(
        (jnp.einsum("nhi,nhj->hij", keys, vals, precision=high), jnp.sum(keys, axis=0)), "kv"
    )
    normed_q = normalize(query_rows).astype(jnp.bfloat16)
    qfeat = feature(jnp.dot(normed_q, w_query, preferred_element_type=jnp.float32)).reshape(
        count, H, DH
    )
    numer = jnp.einsum("nhi,hij->nhj", qfeat, memory, precision=high)
    denom = jnp.einsum("nhi,hi->nh", qfeat, ksum, precision=high)
    attn = (numer / denom[:, :, None]).reshape(count, D).astype(jnp.bfloat16)
    resid = (
        query_rows.astype(jnp.float32) + jnp.dot(attn, w_out, preferred_element_type=jnp.float32)
    ).astype(jnp.bfloat16)
    experts = routes[0, :, 0]
    total_experts = gate_geo.shape[0]
    served = expert_in.shape[0]
    owners = total_experts // served
    onehot = (experts[:, None] == jnp.arange(total_experts, dtype=jnp.int32)[None, :]).astype(
        jnp.int32
    )
    before = jnp.cumsum(onehot, axis=0) - onehot
    rank = jnp.sum(before * onehot, axis=1)
    slot = experts * CAP + rank
    slots_all = total_experts * CAP
    select = (slot[None, :] == jnp.arange(slots_all, dtype=jnp.int32)[:, None]).astype(jnp.bfloat16)
    packed = jnp.dot(
        select, resid.reshape(tiles_here, TILE * D), preferred_element_type=jnp.float32
    ).astype(jnp.bfloat16)
    received = lax.all_to_all(packed, "ex", split_axis=0, concat_axis=0, tiled=True)
    arranged = received.reshape(owners, served, CAP * TILE, D)
    first_layer, second_layer = fetch_rows(expert_in, expert_out)
    outputs = []
    for local in range(served):
        rows = arranged[:, local].reshape(owners * CAP * TILE, D)
        rows = normalize(rows).astype(jnp.bfloat16)
        hidden = jax.nn.gelu(
            jnp.dot(rows, first_layer[local], preferred_element_type=jnp.float32), approximate=False
        ).astype(jnp.bfloat16)
        answer = jnp.dot(hidden, second_layer[local], preferred_element_type=jnp.float32).astype(
            jnp.bfloat16
        )
        outputs.append(answer.reshape(owners, 1, CAP * TILE, D))
    served_out = jnp.concatenate(outputs, axis=1).reshape(slots_all, TILE * D)
    returned = lax.all_to_all(served_out, "ex", split_axis=0, concat_axis=0, tiled=True)
    ffn = jnp.dot(jnp.transpose(select), returned, preferred_element_type=jnp.float32).reshape(
        count, D
    )
    coeff = jnp.dot(onehot.astype(jnp.float32), gate_geo, precision=high)
    logit = jnp.sum(
        coords[0].reshape(3, tiles_here, TILE) * jnp.transpose(coeff)[:, :, None], axis=0
    ).reshape(count)
    gate = jax.nn.sigmoid(logit)
    result = (resid.astype(jnp.float32) + gate[:, None] * ffn).astype(jnp.bfloat16)
    return result[None]


def gelu_exact(x):
    size = jnp.abs(x)
    t = 1.0 / (1.0 + 0.2316418882663604 * size)
    poly = t * (
        0.127414796 + t * (-0.142248368 + t * (0.710706871 + t * (-0.726576014 + t * 0.530702715)))
    )
    return jnp.maximum(x, 0.0) - size * poly * jnp.exp(-0.5 * x * x)


def phi(t):
    return jnp.where(t > 0.0, t + 1.0, jnp.exp(jnp.minimum(t, 0.0)))


def row_norm(rows):
    rows = rows.astype(jnp.float32)
    width = rows.shape[-1]
    centre = rows - jnp.sum(rows, axis=-1, keepdims=True) * (1.0 / width)
    var = jnp.sum(centre * centre, axis=-1, keepdims=True) * (1.0 / width)
    return (centre * lax.rsqrt(var + 1e-05)).astype(jnp.bfloat16)


def dot32(a, b):
    return jnp.dot(a, b, preferred_element_type=jnp.float32)


def fused(
    npb, nkv, nex,
    coords_ref, geo_ref, routes_ref, q_hbm, in_hbm, wq_hbm, wk_hbm, wv_hbm, wo_hbm, ein_ref, eout_ref,
    o_ref,
    q_ref, in_ref, wq_ref, wk_ref, wv_ref, wo_ref,
    w1, w2own, w2oth, qf, resid, normed, hidden, acc, msg, kvbd, ksum,
    load_sem, own_sem, ds_, dr_, zs, zr, ys, yr, xs, xr, fxs, fxr, fys, fyr, cs, cr, ms, mr,
):
    P_, Z, X = lax.axis_index("pb"), lax.axis_index("kv"), lax.axis_index("ex")
    mine, cb = P_ // 2, lax.rem(P_, 2)
    cn = 1 - cb
    xn = 1 - X
    srcs = (ein_ref, eout_ref)
    served = ein_ref.shape[0]
    hs = served // 2
    to_y, to_x, to_c = {"pb": lax.rem(P_ + 2, 4)}, {"ex": xn}, {"pb": 2 * mine + cn}

    loads = [
        pltpu.make_async_copy(src, dst, load_sem.at[k])
        for k, (src, dst) in enumerate(
            ((in_hbm, in_ref), (wk_hbm, wk_ref), (wv_hbm, wv_ref), (q_hbm, q_ref), (wq_hbm, wq_ref), (wo_hbm, wo_ref))
        )
    ]
    for load in loads:
        load.start()

    def block(m, x, side, core_bit, z, half=None):
        experts = pl.ds(x * served, served) if half is None else pl.ds(x * served + half * hs, hs)
        if m:
            return (w2own, w2oth)[side].at[experts, core_bit, z]
        y = mine if side == 0 else 1 - mine
        return w1.at[experts, 2 * y + core_bit, z]

    def yblock(m, x, side, core_bit, z, half=None):
        return block(m, x, 1 - side if m else side, core_bit, z, half)

    def rcopy(src, dst, s, r, dev):
        return pltpu.make_async_remote_copy(
            src_ref=src, dst_ref=dst, send_sem=s, recv_sem=r,
            device_id=dev, device_id_type=pl.DeviceIdType.MESH,
        )

    def zof(d):
        return lax.rem(Z + nkv - d, nkv)

    barrier = pltpu.get_barrier_semaphore()
    partners = [to_y, to_x, to_c] + [{"kv": lax.rem(Z + d, nkv)} for d in range(1, nkv)]
    for dev in partners:
        pl.semaphore_signal(barrier, inc=1, device_id=dev, device_id_type=pl.DeviceIdType.MESH)
    pl.semaphore_wait(barrier, len(partners))

    def own_copy(m):
        return pltpu.make_async_copy(srcs[m], block(m, X, 0, cb, Z), own_sem.at[m])

    def z_copy(m, d):
        return rcopy(srcs[m], block(m, X, 0, cb, Z), zs.at[m, d], zr.at[m, d], {"kv": lax.rem(Z + d, nkv)})

    def diag_copy(m):
        b = block(m, xn, 1, cb, Z)
        return rcopy(b, b, ds_.at[m], dr_.at[m], {"kv": lax.rem(Z + 1, nkv)})

    def arrive(m, x, side, core_bit, d, s, r, dev, half=None):
        b = block(m, x, side, core_bit, zof(d), half)
        rcopy(b, b, s, r, dev).wait_recv()

    def to_x_copy(m, d, src=None):
        b = block(m, X, 0, cb, zof(d))
        return rcopy(b if src is None else src, b, xs.at[m, d], xr.at[m, d], to_x)

    def to_y_copy(m, d, src=None):
        b = block(m, X, 0, cb, zof(d))
        return rcopy(b if src is None else src, yblock(m, X, 0, cb, zof(d)), ys.at[m, d], yr.at[m, d], to_y)

    def on_x_copy(m, d):
        b = block(m, X, 1, cb, zof(d), 0)
        return rcopy(b, b, fxs.at[m, d], fxr.at[m, d], to_x)

    def on_y_copy(m, d):
        b = block(m, xn, 0, cb, zof(d), 1)
        return rcopy(b, yblock(m, xn, 0, cb, zof(d), 1), fys.at[m, d], fyr.at[m, d], to_y)

    kinds = ((X, 0), (X, 1), (xn, 0), (xn, 1))

    def core(m, k, d, src=None):
        b = block(m, *kinds[k], cb, zof(d))
        return rcopy(b if src is None else src, b, cs.at[m, k, d], cr.at[m, k, d], to_c)

    def start_z(m):
        own_copy(m).start()
        for d in range(1, nkv):
            z_copy(m, d).start()

    def start_xy(m):
        to_x_copy(m, 0, srcs[m]).start()
        to_y_copy(m, 0, srcs[m]).start()
        core(m, 0, 0, srcs[m]).start()

    by_link = [d for d in range(nkv) if d != 1]

    def f1(m, d):
        arrive(m, X, 0, cb, d, zs.at[m, d], zr.at[m, d], {"kv": lax.rem(Z + d, nkv)})
        to_x_copy(m, d).start()
        to_y_copy(m, d).start()
        core(m, 0, d).start()

    def f2(m, d):
        arrive(m, X, 1, cb, d, ys.at[m, d], yr.at[m, d], to_y)
        if d in by_link:
            on_x_copy(m, d).start()
        core(m, 1, d).start()
        arrive(m, xn, 0, cb, d, xs.at[m, d], xr.at[m, d], to_x)
        if d in by_link:
            on_y_copy(m, d).start()
        core(m, 2, d).start()

    def f3(m, d):
        if d in by_link:
            arrive(m, xn, 1, cb, d, fxs.at[m, d], fxr.at[m, d], to_x, 0)
            arrive(m, xn, 1, cb, d, fys.at[m, d], fyr.at[m, d], to_y, 1)
        else:
            arrive(m, xn, 1, cb, d, ds_.at[m], dr_.at[m], {"kv": lax.rem(Z + 1, nkv)})
        if d == 0 and nkv > 1:
            diag_copy(m).start()
        core(m, 3, d).start()

    def arrive_core(m, ks):
        for d in range(nkv):
            for k in ks:
                arrive(m, *kinds[k], cn, d, cs.at[m, k, d], cr.at[m, k, d], to_c)

    def sent_all(m):
        for d in range(nkv):
            if d:
                z_copy(m, d).wait_send()
            to_x_copy(m, d).wait_send()
            to_y_copy(m, d).wait_send()
            if d in by_link:
                on_x_copy(m, d).wait_send()
                on_y_copy(m, d).wait_send()
            else:
                diag_copy(m).wait_send()
            for k in range(4):
                core(m, k, d).wait_send()

    start_z(0)
    start_xy(0)

    width = q_ref.shape[1]
    for load in loads[:3]:
        load.wait()
    nin = row_norm(in_ref[...])
    keys = phi(dot32(nin, wk_ref[...]))
    vals = dot32(nin, wv_ref[...])
    keys_b, vals_b = keys.astype(jnp.bfloat16), vals.astype(jnp.bfloat16)
    lane = lax.broadcasted_iota(jnp.int32, (DH, 128), 1) // DH
    per = 128 // DH
    rows_kv = DH * (width // 128)
    for t in range(width // 128):
        cols = slice(128 * t, 128 * (t + 1))
        mem = lax.dot_general(
            keys_b[:, cols], vals_b[:, cols], (((0,), (0,)), ((), ())),
            preferred_element_type=jnp.float32,
        )
        total = jnp.zeros((DH, 128), jnp.float32)
        for h in range(per):
            total = jnp.where(lane == h, mem[h * DH : (h + 1) * DH], total)
        msg[0, DH * t : DH * (t + 1), :] = total
        sums = jnp.sum(keys[:, cols], axis=0, keepdims=True)
        msg[0, rows_kv + 8 * t : rows_kv + 8 * (t + 1), :] = jnp.broadcast_to(sums, (8, 128))

    def m_copy(d):
        return rcopy(msg.at[0], msg.at[d], ms.at[d], mr.at[d], {"kv": lax.rem(Z + d, nkv)})

    for d in range(1, nkv):
        m_copy(d).start()

    count = q_ref.shape[0]
    step = 256
    chunks = count // step

    def q_stage(lo, hi):
        @pl.loop(lo, hi)
        def _(i):
            rows = pl.ds(pl.multiple_of(i * step, step), step)
            qf[rows, :] = phi(dot32(row_norm(q_ref[rows, :]), wq_ref[...])).astype(jnp.bfloat16)

    for load in loads[3:]:
        load.wait()
    part = chunks // 4
    f1(0, 1)
    f2(0, 0)
    q_stage(0, part)
    f1(0, 2)
    f2(0, 1)
    start_z(1)
    q_stage(part, 2 * part)
    f1(0, 3)
    start_xy(1)
    q_stage(2 * part, 3 * part)
    f3(0, 0)
    f2(0, 2)
    q_stage(3 * part, chunks)

    for d in range(1, nkv):
        m_copy(d).wait_recv()
    both = msg[0]
    for d in range(1, nkv):
        both = both + msg[d]
    kvbd[...] = jnp.zeros_like(kvbd)
    for t in range(width // 128):
        mem = both[DH * t : DH * (t + 1)]
        for h in range(per):
            r0 = 128 * t + DH * h
            kvbd[r0 : r0 + DH, 128 * t : 128 * (t + 1)] = jnp.where(lane == h, mem, 0.0).astype(jnp.bfloat16)
        ksum[:, 128 * t : 128 * (t + 1)] = both[rows_kv + 8 * t : rows_kv + 8 * (t + 1)]
    same = (
        lax.broadcasted_iota(jnp.int32, (width, width), 0) // DH
        == lax.broadcasted_iota(jnp.int32, (width, width), 1) // DH
    ).astype(jnp.float32).astype(jnp.bfloat16)

    def attn_stage(lo, hi):
        @pl.loop(lo, hi)
        def _(i):
            rows = pl.ds(pl.multiple_of(i * step, step), step)
            f = qf[rows, :]
            numer = dot32(f, kvbd[...])
            denom = dot32((f.astype(jnp.float32) * ksum[0:1, :]).astype(jnp.bfloat16), same)
            attn = (numer / denom).astype(jnp.bfloat16)
            r = (q_ref[rows, :].astype(jnp.float32) + dot32(attn, wo_ref[...])).astype(jnp.bfloat16)
            resid[rows, :] = r
            normed[rows, :] = row_norm(r)

    attn_stage(0, part)
    f1(1, 1)
    f2(0, 3)
    attn_stage(part, 2 * part)
    f3(0, 1)
    f2(1, 0)
    attn_stage(2 * part, 3 * part)
    f1(1, 2)
    f3(0, 2)
    attn_stage(3 * part, chunks)
    f3(0, 3)
    f2(1, 1)
    own_copy(0).wait()
    arrive_core(0, range(4))

    tiles = count // TILE
    fdim = hidden.shape[1]
    wide = 256

    def up_stage(lo, hi):
        @pl.loop(lo, hi)
        def _(i):
            rows = pl.ds(pl.multiple_of(i * TILE, TILE), TILE)
            e = routes_ref[0, i]
            x = normed[rows, :]
            for c in range(fdim // wide):
                w = w1[e, :, :, :, c * wide : (c + 1) * wide].reshape(width, wide)
                hidden[rows, c * wide : (c + 1) * wide] = gelu_exact(dot32(x, w)).astype(jnp.bfloat16)

    near = fdim // 2
    near_cols = pl.ds(pl.multiple_of(mine * near, near), near)
    far_cols = pl.ds(pl.multiple_of((1 - mine) * near, near), near)

    def mid_stage(lo, hi):
        @pl.loop(lo, hi)
        def _(i):
            rows = pl.ds(pl.multiple_of(i * TILE, TILE), TILE)
            acc[rows, :] = dot32(hidden[rows, near_cols], w2own[routes_ref[0, i]].reshape(near, width))

    part = tiles // 8
    up_stage(0, part)
    f1(1, 3)
    up_stage(part, 2 * part)
    f3(1, 0)
    f2(1, 2)
    up_stage(2 * part, 4 * part)
    f2(1, 3)
    up_stage(4 * part, 6 * part)
    f3(1, 1)
    up_stage(6 * part, tiles)
    f3(1, 2)
    own_copy(1).wait()
    arrive_core(1, (0, 2))
    mid_stage(0, tiles // 2)
    f3(1, 3)
    mid_stage(tiles // 2, tiles)
    arrive_core(1, (1, 3))

    def down_stage(lo, hi):
        @pl.loop(lo, hi)
        def _(i):
            start = pl.multiple_of(i * TILE, TILE)
            rows = pl.ds(start, TILE)
            e = routes_ref[0, i]
            ffn = (acc[rows, :] + dot32(hidden[rows, far_cols], w2oth[e].reshape(near, width))).astype(jnp.bfloat16).astype(jnp.float32)
            logit = coords_ref[0, 0:1, rows] * geo_ref[0, e]
            logit = logit + coords_ref[1, 0:1, rows] * geo_ref[1, e]
            logit = logit + coords_ref[2, 0:1, rows] * geo_ref[2, e]
            gate = 1.0 / (1.0 + jnp.exp(-logit))
            gate = jnp.transpose(jnp.broadcast_to(gate, (TILE, TILE)))
            gate = jnp.concatenate([gate] * (width // TILE), axis=1)
            o_ref[rows, :] = (resid[rows, :].astype(jnp.float32) + gate * ffn).astype(jnp.bfloat16)

    down_stage(0, tiles)

    sent_all(0)
    sent_all(1)
    for d in range(1, nkv):
        m_copy(d).wait_send()


def fused_body(npb, nkv, nex, queries, coords, inputs, w_query, w_key, w_value, w_out, expert_in, expert_out, gate_geo, routes):
    count, width = queries.shape[1:]
    served, rows1, fdim = expert_in.shape
    rows2 = expert_out.shape[1]
    total = served * nex
    vmem = pl.BlockSpec(memory_space=pltpu.VMEM)
    smem = pl.BlockSpec(memory_space=pltpu.SMEM)
    hbm = pl.BlockSpec(memory_space=pl.ANY)
    dma = pltpu.SemaphoreType.DMA
    bf = jnp.bfloat16
    out = pl.pallas_call(
        functools.partial(fused, npb, nkv, nex),
        out_shape=jax.ShapeDtypeStruct((count, width), bf),
        in_specs=[vmem] + [smem] * 2 + [hbm] * 8,
        out_specs=vmem,
        scratch_shapes=[
            pltpu.VMEM((count, width), bf),
            pltpu.VMEM(inputs.shape[1:], bf),
        ] + [pltpu.VMEM((width, width), bf)] * 4 + [
            pltpu.VMEM((total, npb, nkv, rows1, fdim), bf),
            pltpu.VMEM((total, npb // 2, nkv, rows2, width), bf),
            pltpu.VMEM((total, npb // 2, nkv, rows2, width), bf),
            pltpu.VMEM((count, width), bf),
            pltpu.VMEM((count, width), bf),
            pltpu.VMEM((count, width), bf),
            pltpu.VMEM((count, fdim), bf),
            pltpu.VMEM((count, width), jnp.float32),
            pltpu.VMEM((nkv, (DH + 8) * (width // 128), 128), jnp.float32),
            pltpu.VMEM((width, width), bf),
            pltpu.VMEM((8, width), jnp.float32),
            dma((6,)),
        ] + [dma((2,))] * 3 + [dma((2, nkv))] * 10 + [dma((2, 4, nkv))] * 2 + [dma((nkv,))] * 2,
        compiler_params=pltpu.CompilerParams(collective_id=0, has_side_effects=True),
        name="fused",
    )(
        jnp.transpose(coords, (1, 0, 2)), jnp.transpose(gate_geo), routes[:, :, 0],
        queries[0], inputs[0], w_query, w_key, w_value, w_out, expert_in, expert_out,
    )
    return out[None]


def solution(mesh):
    in_specs = (
        P(("pb", "ex"), "kv", None),
        P(("pb", "ex"), None, "kv"),
        P(("pb", "ex"), "kv", None),
        P(),
        P(),
        P(),
        P(),
        P("ex", ("pb", "kv"), None),
        P("ex", ("pb", "kv"), None),
        P(),
        P(("pb", "ex"), "kv", None),
    )
    out_specs = P(("pb", "ex"), "kv", None)
    npb, nkv, nex = (mesh.shape[a] for a in ("pb", "kv", "ex"))
    chosen = functools.partial(fused_body, npb, nkv, nex) if (npb, nex) == (4, 2) else body
    return jax.shard_map(chosen, mesh=mesh, in_specs=in_specs, out_specs=out_specs, check_vma=False)
```

```python
import functools

import jax
import jax.numpy as jnp
from jax import lax
from jax.experimental import pallas as pl
from jax.experimental.pallas import tpu as pltpu
from jax.sharding import PartitionSpec as P

D = 256
H = 8
DH = 32
TILE = 128
CAP = 3


def normalize(rows):
    rows = rows.astype(jnp.float32)
    centre = rows - jnp.mean(rows, axis=-1, keepdims=True)
    return centre * lax.rsqrt(jnp.mean(centre * centre, axis=-1, keepdims=True) + 1e-05)


def feature(values):
    return jax.nn.elu(values) + 1.0


def fetch_rows(expert_in, expert_out):
    return (
        lax.all_gather(expert_in, ("pb", "kv"), axis=1, tiled=True),
        lax.all_gather(expert_out, ("pb", "kv"), axis=1, tiled=True),
    )


def body(
    queries, coords, inputs, w_query, w_key, w_value, w_out, expert_in, expert_out, gate_geo, routes
):
    high = lax.Precision.HIGHEST
    query_rows = queries[0]
    count = query_rows.shape[0]
    tiles_here = count // TILE
    normed_in = normalize(inputs[0]).astype(jnp.bfloat16)
    points = normed_in.shape[0]
    keys = feature(jnp.dot(normed_in, w_key, preferred_element_type=jnp.float32)).reshape(
        points, H, DH
    )
    vals = jnp.dot(normed_in, w_value, preferred_element_type=jnp.float32).reshape(points, H, DH)
    memory, ksum = lax.psum(
        (jnp.einsum("nhi,nhj->hij", keys, vals, precision=high), jnp.sum(keys, axis=0)), "kv"
    )
    normed_q = normalize(query_rows).astype(jnp.bfloat16)
    qfeat = feature(jnp.dot(normed_q, w_query, preferred_element_type=jnp.float32)).reshape(
        count, H, DH
    )
    numer = jnp.einsum("nhi,hij->nhj", qfeat, memory, precision=high)
    denom = jnp.einsum("nhi,hi->nh", qfeat, ksum, precision=high)
    attn = (numer / denom[:, :, None]).reshape(count, D).astype(jnp.bfloat16)
    resid = (
        query_rows.astype(jnp.float32) + jnp.dot(attn, w_out, preferred_element_type=jnp.float32)
    ).astype(jnp.bfloat16)
    experts = routes[0, :, 0]
    total_experts = gate_geo.shape[0]
    served = expert_in.shape[0]
    owners = total_experts // served
    onehot = (experts[:, None] == jnp.arange(total_experts, dtype=jnp.int32)[None, :]).astype(
        jnp.int32
    )
    before = jnp.cumsum(onehot, axis=0) - onehot
    rank = jnp.sum(before * onehot, axis=1)
    slot = experts * CAP + rank
    slots_all = total_experts * CAP
    select = (slot[None, :] == jnp.arange(slots_all, dtype=jnp.int32)[:, None]).astype(jnp.bfloat16)
    packed = jnp.dot(
        select, resid.reshape(tiles_here, TILE * D), preferred_element_type=jnp.float32
    ).astype(jnp.bfloat16)
    received = lax.all_to_all(packed, "ex", split_axis=0, concat_axis=0, tiled=True)
    arranged = received.reshape(owners, served, CAP * TILE, D)
    first_layer, second_layer = fetch_rows(expert_in, expert_out)
    outputs = []
    for local in range(served):
        rows = arranged[:, local].reshape(owners * CAP * TILE, D)
        rows = normalize(rows).astype(jnp.bfloat16)
        hidden = jax.nn.gelu(
            jnp.dot(rows, first_layer[local], preferred_element_type=jnp.float32), approximate=False
        ).astype(jnp.bfloat16)
        answer = jnp.dot(hidden, second_layer[local], preferred_element_type=jnp.float32).astype(
            jnp.bfloat16
        )
        outputs.append(answer.reshape(owners, 1, CAP * TILE, D))
    served_out = jnp.concatenate(outputs, axis=1).reshape(slots_all, TILE * D)
    returned = lax.all_to_all(served_out, "ex", split_axis=0, concat_axis=0, tiled=True)
    ffn = jnp.dot(jnp.transpose(select), returned, preferred_element_type=jnp.float32).reshape(
        count, D
    )
    coeff = jnp.dot(onehot.astype(jnp.float32), gate_geo, precision=high)
    logit = jnp.sum(
        coords[0].reshape(3, tiles_here, TILE) * jnp.transpose(coeff)[:, :, None], axis=0
    ).reshape(count)
    gate = jax.nn.sigmoid(logit)
    result = (resid.astype(jnp.float32) + gate[:, None] * ffn).astype(jnp.bfloat16)
    return result[None]


def gelu_exact(x):
    size = jnp.abs(x)
    t = 1.0 / (1.0 + 0.2316418882663604 * size)
    poly = t * (
        0.127414796 + t * (-0.142248368 + t * (0.710706871 + t * (-0.726576014 + t * 0.530702715)))
    )
    return jnp.maximum(x, 0.0) - size * poly * jnp.exp(-0.5 * x * x)


def phi(t):
    return jnp.where(t > 0.0, t + 1.0, jnp.exp(jnp.minimum(t, 0.0)))


def row_norm(rows):
    rows = rows.astype(jnp.float32)
    width = rows.shape[-1]
    centre = rows - jnp.sum(rows, axis=-1, keepdims=True) * (1.0 / width)
    var = jnp.sum(centre * centre, axis=-1, keepdims=True) * (1.0 / width)
    return (centre * lax.rsqrt(var + 1e-05)).astype(jnp.bfloat16)


def dot32(a, b):
    return jnp.dot(a, b, preferred_element_type=jnp.float32)


def fused(
    npb, nkv, nex,
    coords_ref, geo_ref, routes_ref, q_hbm, in_hbm, wq_hbm, wk_hbm, wv_hbm, wo_hbm, ein_ref, eout_ref,
    o_ref,
    q_ref, in_ref, wq_ref, wk_ref, wv_ref, wo_ref,
    w1, w2own, w2oth, qf, resid, normed, hidden, acc, msg, kvbd, ksum,
    load_sem, own_sem, zs, zr, ys, yr, xs, xr, fxs, fxr, fys, fyr, cs, cr, ms, mr,
):
    P_, Z, X = lax.axis_index("pb"), lax.axis_index("kv"), lax.axis_index("ex")
    mine, cb = P_ // 2, lax.rem(P_, 2)
    cn = 1 - cb
    xn = 1 - X
    srcs = (ein_ref, eout_ref)
    served = ein_ref.shape[0]
    hs = served // 2
    to_y, to_x, to_c = {"pb": lax.rem(P_ + 2, 4)}, {"ex": xn}, {"pb": 2 * mine + cn}

    loads = [
        pltpu.make_async_copy(src, dst, load_sem.at[k])
        for k, (src, dst) in enumerate(
            ((in_hbm, in_ref), (wk_hbm, wk_ref), (wv_hbm, wv_ref), (q_hbm, q_ref), (wq_hbm, wq_ref), (wo_hbm, wo_ref))
        )
    ]
    for load in loads:
        load.start()

    def block(m, x, side, core_bit, z, half=None):
        experts = pl.ds(x * served, served) if half is None else pl.ds(x * served + half * hs, hs)
        if m:
            return (w2own, w2oth)[side].at[experts, core_bit, z]
        y = mine if side == 0 else 1 - mine
        return w1.at[experts, 2 * y + core_bit, z]

    def yblock(m, x, side, core_bit, z, half=None):
        return block(m, x, 1 - side if m else side, core_bit, z, half)

    def rcopy(src, dst, s, r, dev):
        return pltpu.make_async_remote_copy(
            src_ref=src, dst_ref=dst, send_sem=s, recv_sem=r,
            device_id=dev, device_id_type=pl.DeviceIdType.MESH,
        )

    def zof(d):
        return lax.rem(Z + nkv - d, nkv)

    barrier = pltpu.get_barrier_semaphore()
    partners = [to_y, to_x, to_c] + [{"kv": lax.rem(Z + d, nkv)} for d in range(1, nkv)]
    for dev in partners:
        pl.semaphore_signal(barrier, inc=1, device_id=dev, device_id_type=pl.DeviceIdType.MESH)
    pl.semaphore_wait(barrier, len(partners))

    def own_copy(m):
        return pltpu.make_async_copy(srcs[m], block(m, X, 0, cb, Z), own_sem.at[m])

    def z_copy(m, d):
        return rcopy(srcs[m], block(m, X, 0, cb, Z), zs.at[m, d], zr.at[m, d], {"kv": lax.rem(Z + d, nkv)})

    def arrive(m, x, side, core_bit, d, s, r, dev, half=None):
        b = block(m, x, side, core_bit, zof(d), half)
        rcopy(b, b, s, r, dev).wait_recv()

    def to_x_copy(m, d, src=None):
        b = block(m, X, 0, cb, zof(d))
        return rcopy(b if src is None else src, b, xs.at[m, d], xr.at[m, d], to_x)

    def to_y_copy(m, d, src=None):
        b = block(m, X, 0, cb, zof(d))
        return rcopy(b if src is None else src, yblock(m, X, 0, cb, zof(d)), ys.at[m, d], yr.at[m, d], to_y)

    def on_x_copy(m, d):
        b = block(m, X, 1, cb, zof(d), 0)
        return rcopy(b, b, fxs.at[m, d], fxr.at[m, d], to_x)

    def on_y_copy(m, d):
        b = block(m, xn, 0, cb, zof(d), 1)
        return rcopy(b, yblock(m, xn, 0, cb, zof(d), 1), fys.at[m, d], fyr.at[m, d], to_y)

    kinds = ((X, 0), (X, 1), (xn, 0), (xn, 1))

    def core(m, k, d, src=None):
        b = block(m, *kinds[k], cb, zof(d))
        return rcopy(b if src is None else src, b, cs.at[m, k, d], cr.at[m, k, d], to_c)

    def start_z(m):
        own_copy(m).start()
        for d in range(1, nkv):
            z_copy(m, d).start()

    def start_xy(m):
        to_x_copy(m, 0, srcs[m]).start()
        to_y_copy(m, 0, srcs[m]).start()
        core(m, 0, 0, srcs[m]).start()

    def f1(m, d):
        arrive(m, X, 0, cb, d, zs.at[m, d], zr.at[m, d], {"kv": lax.rem(Z + d, nkv)})
        to_x_copy(m, d).start()
        to_y_copy(m, d).start()
        core(m, 0, d).start()

    def f2(m, d):
        arrive(m, X, 1, cb, d, ys.at[m, d], yr.at[m, d], to_y)
        on_x_copy(m, d).start()
        core(m, 1, d).start()
        arrive(m, xn, 0, cb, d, xs.at[m, d], xr.at[m, d], to_x)
        on_y_copy(m, d).start()
        core(m, 2, d).start()

    def f3(m, d):
        arrive(m, xn, 1, cb, d, fxs.at[m, d], fxr.at[m, d], to_x, 0)
        arrive(m, xn, 1, cb, d, fys.at[m, d], fyr.at[m, d], to_y, 1)
        core(m, 3, d).start()

    def arrive_core(m, ks):
        for d in range(nkv):
            for k in ks:
                arrive(m, *kinds[k], cn, d, cs.at[m, k, d], cr.at[m, k, d], to_c)

    def sent_all(m):
        for d in range(nkv):
            if d:
                z_copy(m, d).wait_send()
            to_x_copy(m, d).wait_send()
            to_y_copy(m, d).wait_send()
            on_x_copy(m, d).wait_send()
            on_y_copy(m, d).wait_send()
            for k in range(4):
                core(m, k, d).wait_send()

    start_z(0)
    start_xy(0)

    width = q_ref.shape[1]
    for load in loads[:3]:
        load.wait()
    nin = row_norm(in_ref[...])
    keys = phi(dot32(nin, wk_ref[...]))
    vals = dot32(nin, wv_ref[...])
    keys_b, vals_b = keys.astype(jnp.bfloat16), vals.astype(jnp.bfloat16)
    lane = lax.broadcasted_iota(jnp.int32, (DH, 128), 1) // DH
    per = 128 // DH
    rows_kv = DH * (width // 128)
    for t in range(width // 128):
        cols = slice(128 * t, 128 * (t + 1))
        mem = lax.dot_general(
            keys_b[:, cols], vals_b[:, cols], (((0,), (0,)), ((), ())),
            preferred_element_type=jnp.float32,
        )
        total = jnp.zeros((DH, 128), jnp.float32)
        for h in range(per):
            total = jnp.where(lane == h, mem[h * DH : (h + 1) * DH], total)
        msg[0, DH * t : DH * (t + 1), :] = total
        sums = jnp.sum(keys[:, cols], axis=0, keepdims=True)
        msg[0, rows_kv + 8 * t : rows_kv + 8 * (t + 1), :] = jnp.broadcast_to(sums, (8, 128))

    def m_copy(d):
        return rcopy(msg.at[0], msg.at[d], ms.at[d], mr.at[d], {"kv": lax.rem(Z + d, nkv)})

    for d in range(1, nkv):
        m_copy(d).start()

    count = q_ref.shape[0]
    step = 256
    chunks = count // step

    def q_stage(lo, hi):
        @pl.loop(lo, hi)
        def _(i):
            rows = pl.ds(pl.multiple_of(i * step, step), step)
            qf[rows, :] = phi(dot32(row_norm(q_ref[rows, :]), wq_ref[...])).astype(jnp.bfloat16)

    for load in loads[3:]:
        load.wait()
    part = chunks // 4
    f1(0, 1)
    f2(0, 0)
    q_stage(0, part)
    f1(0, 2)
    f2(0, 1)
    start_z(1)
    q_stage(part, 2 * part)
    f1(0, 3)
    start_xy(1)
    q_stage(2 * part, 3 * part)
    f3(0, 0)
    f2(0, 2)
    q_stage(3 * part, chunks)

    for d in range(1, nkv):
        m_copy(d).wait_recv()
    both = msg[0]
    for d in range(1, nkv):
        both = both + msg[d]
    kvbd[...] = jnp.zeros_like(kvbd)
    for t in range(width // 128):
        mem = both[DH * t : DH * (t + 1)]
        for h in range(per):
            r0 = 128 * t + DH * h
            kvbd[r0 : r0 + DH, 128 * t : 128 * (t + 1)] = jnp.where(lane == h, mem, 0.0).astype(jnp.bfloat16)
        ksum[:, 128 * t : 128 * (t + 1)] = both[rows_kv + 8 * t : rows_kv + 8 * (t + 1)]
    same = (
        lax.broadcasted_iota(jnp.int32, (width, width), 0) // DH
        == lax.broadcasted_iota(jnp.int32, (width, width), 1) // DH
    ).astype(jnp.float32).astype(jnp.bfloat16)

    def attn_stage(lo, hi):
        @pl.loop(lo, hi)
        def _(i):
            rows = pl.ds(pl.multiple_of(i * step, step), step)
            f = qf[rows, :]
            numer = dot32(f, kvbd[...])
            denom = dot32((f.astype(jnp.float32) * ksum[0:1, :]).astype(jnp.bfloat16), same)
            attn = (numer / denom).astype(jnp.bfloat16)
            r = (q_ref[rows, :].astype(jnp.float32) + dot32(attn, wo_ref[...])).astype(jnp.bfloat16)
            resid[rows, :] = r
            normed[rows, :] = row_norm(r)

    attn_stage(0, part)
    f1(1, 1)
    f2(0, 3)
    attn_stage(part, 2 * part)
    f3(0, 1)
    f2(1, 0)
    attn_stage(2 * part, 3 * part)
    f1(1, 2)
    f3(0, 2)
    attn_stage(3 * part, chunks)
    f3(0, 3)
    f2(1, 1)
    f1(1, 3)
    own_copy(0).wait()
    arrive_core(0, range(4))

    tiles = count // TILE
    fdim = hidden.shape[1]
    wide = 256

    def up_stage(lo, hi):
        @pl.loop(lo, hi)
        def _(i):
            rows = pl.ds(pl.multiple_of(i * TILE, TILE), TILE)
            e = routes_ref[0, i]
            x = normed[rows, :]
            for c in range(fdim // wide):
                w = w1[e, :, :, :, c * wide : (c + 1) * wide].reshape(width, wide)
                hidden[rows, c * wide : (c + 1) * wide] = gelu_exact(dot32(x, w)).astype(jnp.bfloat16)

    near = fdim // 2
    near_cols = pl.ds(pl.multiple_of(mine * near, near), near)
    far_cols = pl.ds(pl.multiple_of((1 - mine) * near, near), near)

    def mid_stage(lo, hi):
        @pl.loop(lo, hi)
        def _(i):
            rows = pl.ds(pl.multiple_of(i * TILE, TILE), TILE)
            acc[rows, :] = dot32(hidden[rows, near_cols], w2own[routes_ref[0, i]].reshape(near, width))

    part = tiles // 8
    up_stage(0, part)
    f3(1, 0)
    up_stage(part, 2 * part)
    f2(1, 2)
    up_stage(2 * part, 4 * part)
    f2(1, 3)
    up_stage(4 * part, 5 * part)
    f3(1, 1)
    up_stage(5 * part, 6 * part)
    f3(1, 2)
    up_stage(6 * part, tiles)
    own_copy(1).wait()
    arrive_core(1, (0, 2))
    mid_stage(0, tiles // 2)
    f3(1, 3)
    mid_stage(tiles // 2, tiles)
    arrive_core(1, (1, 3))

    def down_stage(lo, hi):
        @pl.loop(lo, hi)
        def _(i):
            start = pl.multiple_of(i * TILE, TILE)
            rows = pl.ds(start, TILE)
            e = routes_ref[0, i]
            ffn = (acc[rows, :] + dot32(hidden[rows, far_cols], w2oth[e].reshape(near, width))).astype(jnp.bfloat16).astype(jnp.float32)
            logit = coords_ref[0, 0:1, rows] * geo_ref[0, e]
            logit = logit + coords_ref[1, 0:1, rows] * geo_ref[1, e]
            logit = logit + coords_ref[2, 0:1, rows] * geo_ref[2, e]
            gate = 1.0 / (1.0 + jnp.exp(-logit))
            gate = jnp.transpose(jnp.broadcast_to(gate, (TILE, TILE)))
            gate = jnp.concatenate([gate] * (width // TILE), axis=1)
            o_ref[rows, :] = (resid[rows, :].astype(jnp.float32) + gate * ffn).astype(jnp.bfloat16)

    down_stage(0, tiles)

    sent_all(0)
    sent_all(1)
    for d in range(1, nkv):
        m_copy(d).wait_send()


def fused_body(npb, nkv, nex, queries, coords, inputs, w_query, w_key, w_value, w_out, expert_in, expert_out, gate_geo, routes):
    count, width = queries.shape[1:]
    served, rows1, fdim = expert_in.shape
    rows2 = expert_out.shape[1]
    total = served * nex
    vmem = pl.BlockSpec(memory_space=pltpu.VMEM)
    smem = pl.BlockSpec(memory_space=pltpu.SMEM)
    hbm = pl.BlockSpec(memory_space=pl.ANY)
    dma = pltpu.SemaphoreType.DMA
    bf = jnp.bfloat16
    out = pl.pallas_call(
        functools.partial(fused, npb, nkv, nex),
        out_shape=jax.ShapeDtypeStruct((count, width), bf),
        in_specs=[vmem] + [smem] * 2 + [hbm] * 8,
        out_specs=vmem,
        scratch_shapes=[
            pltpu.VMEM((count, width), bf),
            pltpu.VMEM(inputs.shape[1:], bf),
        ] + [pltpu.VMEM((width, width), bf)] * 4 + [
            pltpu.VMEM((total, npb, nkv, rows1, fdim), bf),
            pltpu.VMEM((total, npb // 2, nkv, rows2, width), bf),
            pltpu.VMEM((total, npb // 2, nkv, rows2, width), bf),
            pltpu.VMEM((count, width), bf),
            pltpu.VMEM((count, width), bf),
            pltpu.VMEM((count, width), bf),
            pltpu.VMEM((count, fdim), bf),
            pltpu.VMEM((count, width), jnp.float32),
            pltpu.VMEM((nkv, (DH + 8) * (width // 128), 128), jnp.float32),
            pltpu.VMEM((width, width), bf),
            pltpu.VMEM((8, width), jnp.float32),
            dma((6,)),
        ] + [dma((2,))] + [dma((2, nkv))] * 10 + [dma((2, 4, nkv))] * 2 + [dma((nkv,))] * 2,
        compiler_params=pltpu.CompilerParams(collective_id=0, has_side_effects=True),
        name="fused",
    )(
        jnp.transpose(coords, (1, 0, 2)), jnp.transpose(gate_geo), routes[:, :, 0],
        queries[0], inputs[0], w_query, w_key, w_value, w_out, expert_in, expert_out,
    )
    return out[None]


def solution(mesh):
    in_specs = (
        P(("pb", "ex"), "kv", None),
        P(("pb", "ex"), None, "kv"),
        P(("pb", "ex"), "kv", None),
        P(),
        P(),
        P(),
        P(),
        P("ex", ("pb", "kv"), None),
        P("ex", ("pb", "kv"), None),
        P(),
        P(("pb", "ex"), "kv", None),
    )
    out_specs = P(("pb", "ex"), "kv", None)
    npb, nkv, nex = (mesh.shape[a] for a in ("pb", "kv", "ex"))
    chosen = functools.partial(fused_body, npb, nkv, nex) if (npb, nex) == (4, 2) else body
    return jax.shard_map(chosen, mesh=mesh, in_specs=in_specs, out_specs=out_specs, check_vma=False)
```
